32 devices in a mesh: ctx: 16 (over z, y, x), kv: 2 (over core).
Axes of the slice: x: 2, y: 2, z: 4, core: 2. Of those that a mesh axis runs over, the one named last changes fastest.
Arguments:
- query_rows: bfloat16 [8192, 1024], P('ctx'), may hold values from -4.5 to 4.5
- key_rows: bfloat16 [8192, 128], P(('ctx', 'kv')), may hold values from -4.5 to 4.5
- value_rows: bfloat16 [8192, 128], P(('ctx', 'kv')), may hold values from -6 to 6
- doc_ids: int32 [8192], P('ctx'), may hold values from 0 to 7, never falling along the last dimension, each value on 1 to 2048 neighbouring positions
Outputs:
- attended: bfloat16 [8192, 1024], P('ctx')
The draws below stay inside these ranges and needn't reach their ends.
Inputs may be any that keep to these rules, and one draw needn't show every extreme that they name: `doc_ids`: non-decreasing; every document has 1 to 2048 tokens and one has exactly 2048.
All inputs are finite; a program needn't handle non-finite values.
Results may differ from the reference program's by a relative error of at most 0.0045.
Values may be sent and summed in bfloat16 or wider, within the bound.
No kernel may reach another device: no remote copies, remote signals or barrier semaphores. Data moves between devices by JAX's collectives and lax.ppermute only.
A program may use at most 64 MiB of HBM per device.

```python
import math
import jax
import jax.numpy as jnp
import numpy as np
from jax import lax

S_DEV = 512
HEADS = 8
HEAD_DIM = 128
DOC_MAX = 2048
TOKENS = 8192
DOCS = 8
N_CTX = 16


def draw_key_rows(key, part):
    noise = jax.random.normal(jax.random.fold_in(key, 11), (TOKENS, HEAD_DIM), jnp.float32)
    return jnp.clip(noise, -4.5, 4.5).astype(jnp.bfloat16)


def draw_query_rows(key, part):
    noise = jax.random.normal(jax.random.fold_in(key, 21), (TOKENS, HEADS * HEAD_DIM), jnp.float32)
    return jnp.clip(noise, -4.5, 4.5).astype(jnp.bfloat16)


def draw_value_rows(key, part):
    noise = jax.random.normal(jax.random.fold_in(key, 31), (TOKENS, HEAD_DIM), jnp.float32)
    return jnp.clip(noise, -6.0, 6.0).astype(jnp.bfloat16)


def split_up(number_of, total, reach, skew):
    loads = [(1 << 20) // math.isqrt(rank ** skew) + 1 for rank in range(2, number_of + 1)]
    surplus, holding = total - reach - (number_of - 1), [1] * (number_of - 1)
    while surplus > 0:
        free = [i for i in range(number_of - 1) if holding[i] < reach]
        whole, left = sum([loads[i] for i in free]), surplus
        for i in free:
            extra = min(reach - holding[i], max(1, left * loads[i] // whole), surplus)
            holding[i] = holding[i] + extra
            surplus = surplus - extra
    return np.array([reach] + holding)


def ragged_sizes(key, amount, total, limit, lean):
    if amount == 2:
        one = jax.random.randint(key, (), max(1, total - limit), min(limit, total - 1) + 1)
        return jnp.stack([one, total - one])
    lengths = jnp.asarray(split_up(amount, total, limit, lean), jnp.int32)
    twos = (amount - 1) // 2
    source_of, receiver = lengths[1:1 + 2 * twos:2], lengths[2:2 + 2 * twos:2]
    room = jnp.minimum(source_of - 1, limit - receiver)
    moved = jax.random.randint(jax.random.fold_in(key, 1), (twos,), 0, 1 << 20) % (room + 1)
    lengths = lengths.at[1:1 + 2 * twos:2].set(source_of - moved).at[2:2 + 2 * twos:2].set(receiver + moved)
    return lengths[jax.random.permutation(jax.random.fold_in(key, 2), amount)]


def setup_inputs(seed: int = 0) -> dict:
    splits = jax.random.split(jax.random.key(seed), 5)
    query_rows = draw_query_rows(jax.random.fold_in(splits[4], 71), 0)
    key_rows = draw_key_rows(jax.random.fold_in(splits[4], 71), 0)
    value_rows = draw_value_rows(jax.random.fold_in(splits[4], 71), 0)
    doc_ids = jnp.searchsorted(jnp.cumsum(ragged_sizes(splits[3], DOCS, TOKENS, DOC_MAX, 0)), jnp.arange(TOKENS), side="right").astype(jnp.int32)
    return {"query_rows": query_rows, "key_rows": key_rows, "value_rows": value_rows, "doc_ids": doc_ids}


floor_score = -1e+30

def reference(query_rows, key_rows, value_rows, doc_ids):
    score_scale = 1.0 / math.sqrt(HEAD_DIM)
    window = DOC_MAX + S_DEV
    padded_keys = jnp.concatenate([jnp.zeros((DOC_MAX, HEAD_DIM), key_rows.dtype), key_rows], 0)
    padded_values = jnp.concatenate([jnp.zeros((DOC_MAX, HEAD_DIM), value_rows.dtype), value_rows], 0)
    padded_ids = jnp.concatenate([jnp.full((DOC_MAX,), -1, jnp.int32), doc_ids.astype(jnp.int32)], 0)

    def one_block(index):
        start = (index * S_DEV).astype(jnp.int32)
        queries = lax.dynamic_slice_in_dim(query_rows, start, S_DEV, 0).reshape(S_DEV, HEADS, HEAD_DIM).astype(jnp.float32)
        keys_here = lax.dynamic_slice_in_dim(padded_keys, start, window, 0).astype(jnp.float32)
        values_here = lax.dynamic_slice_in_dim(padded_values, start, window, 0).astype(jnp.float32)
        key_ids = lax.dynamic_slice_in_dim(padded_ids, start, window, 0)
        query_ids = lax.dynamic_slice_in_dim(doc_ids.astype(jnp.int32), start, S_DEV, 0)
        query_pos = start + jnp.arange(S_DEV, dtype=jnp.int32)
        key_pos = start - DOC_MAX + jnp.arange(window, dtype=jnp.int32)
        visible = (query_ids[:, None] == key_ids[None, :]) & (key_pos[None, :] <= query_pos[:, None])
        scores = jnp.einsum('qhd,kd->qhk', queries, keys_here) * score_scale
        scores = jnp.where(visible[:, None, :], scores, floor_score)
        largest = lax.optimization_barrier(jnp.max(scores, -1))
        weights = jnp.where(visible[:, None, :], jnp.exp(scores - largest[..., None]), 0.0)
        total = lax.optimization_barrier(jnp.sum(weights, -1))
        rounded = lax.optimization_barrier(weights.astype(jnp.bfloat16))
        mixed = jnp.einsum('qhk,kd->qhd', rounded.astype(jnp.float32), values_here)
        return (mixed / total[..., None]).astype(jnp.bfloat16).reshape(S_DEV, HEADS * HEAD_DIM)
    blocks = lax.map(one_block, jnp.arange(N_CTX, dtype=jnp.int32))
    return blocks.reshape(TOKENS, HEADS * HEAD_DIM)
```

```python
import functools
import math

import jax
import jax.numpy as jnp
from jax import lax
from jax.experimental import pallas as pl
from jax.experimental.pallas import tpu as pltpu
from jax.sharding import PartitionSpec as P

HEADS = 8
HEAD_DIM = 128
ID_ROWS = 16
TOTAL_ROWS = 16
STAT_ROWS = 32
GROUP = 3
floor_score = -1e30
SCORE_SCALE = math.log2(math.e) / math.sqrt(HEAD_DIM)


VMEM = pl.BlockSpec(memory_space=pltpu.VMEM)


def pack_kernel(key_ref, value_ref, ids_ref, pack_ref):
    key_count = key_ref.shape[0]
    pack_ref[:key_count, :HEAD_DIM] = key_ref[...]
    pack_ref[:key_count, HEAD_DIM:] = value_ref[...]
    lane_rows = key_count // 128
    first = lax.axis_index("kv") * lane_rows
    ids = ids_ref[...]
    half = jnp.where(first == 0, ids[:lane_rows], ids[lane_rows : 2 * lane_rows])
    row = jnp.concatenate([half[i : i + 1] for i in range(lane_rows)], axis=1)
    row = row.astype(jnp.float32).astype(jnp.bfloat16)
    pack_ref[key_count:, :] = jnp.broadcast_to(row, (ID_ROWS, key_count))


def softmax_step(scores, values, held_refs, mixed_ref, large_ref, h, cols, column_valid):
    fresh = held_refs is None
    largest = functools.reduce(
        jnp.maximum, [jnp.max(block, axis=0, keepdims=True) for block in scores]
    )
    largest = largest * SCORE_SCALE
    if not fresh:
        held = held_refs[1][h, :, cols]
        largest = jnp.maximum(held, largest)
        if column_valid is not None:
            largest = jnp.where(column_valid, largest, held)
    shift = largest
    if column_valid is not None:
        shift = jnp.where(column_valid, largest, -floor_score)
    weights = jnp.concatenate(
        [jnp.exp2(block * SCORE_SCALE - shift).astype(jnp.bfloat16) for block in scores], axis=0
    )
    update = jnp.dot(values, weights, preferred_element_type=jnp.float32)
    if fresh:
        mixed_ref[h, :, cols] = update
    else:
        factor = jnp.exp2(held - largest)
        mixed_ref[h, :, cols] = held_refs[0][h, :, cols] * factor + update
    large_ref[h, :, cols] = largest


def own_kernel(query_ref, pack_ref, ids_ref, turned_ref, mixed_ref, large_ref, value_ref, bias_ref):
    rows = query_ref.shape[0]
    key_count = pack_ref.shape[1]
    for h in range(HEADS):
        turned_ref[h] = query_ref[:, h * HEAD_DIM : (h + 1) * HEAD_DIM].T
    value_ref[:HEAD_DIM] = pack_ref[:key_count, HEAD_DIM:].T
    value_ref[HEAD_DIM:] = jnp.ones((TOTAL_ROWS, key_count), jnp.bfloat16)
    ids = ids_ref[...].astype(jnp.float32)
    token_ids = jnp.concatenate([ids[i : i + 1] for i in range(rows // 128)], axis=1)
    row = pack_ref[key_count:, :][:1].astype(jnp.float32)
    key_ids = jnp.broadcast_to(row, (128, key_count)).T[:, :1]
    token_pos = lax.broadcasted_iota(jnp.int32, (key_count, rows), 1)
    key_pos = lax.broadcasted_iota(jnp.int32, (key_count, rows), 0)
    key_pos = key_pos + lax.axis_index("kv") * key_count
    visible = (key_ids == token_ids) & (key_pos <= token_pos)
    bias_ref[...] = jnp.where(visible, 0.0, floor_score)
    cols = pl.ds(0, rows)

    def one(step, carry):
        for u in range(2):
            h = step * 2 + u
            scores = jnp.dot(
                pack_ref[:key_count, :HEAD_DIM], turned_ref[h], preferred_element_type=jnp.float32
            )
            scores = scores + bias_ref[...]
            softmax_step([scores], value_ref[...], None, mixed_ref, large_ref, h, cols, None)
        return carry

    lax.fori_loop(0, HEADS // 2, one, 0)


def behind_kernel(*refs, distances, final):
    count = len(distances)
    turned_ref, ids_ref = refs[:2]
    chunks = refs[2 : 2 + count]
    held_refs = refs[2 + count : 4 + count]
    rest = refs[4 + count :]
    mixed_ref, large_ref = rest[:2]
    value_ref = rest[-1]
    rows = turned_ref.shape[2]
    key_count = chunks[0].shape[1]
    cycle_index = lax.axis_index("ctx")
    ids = ids_ref[...].astype(jnp.float32)
    first_id = jnp.min(ids)
    run = jnp.sum((ids == first_id).astype(jnp.float32)).astype(jnp.int32)
    starts = []
    for chunk, distance in zip(chunks, distances):
        key_ids = chunk[key_count:, :][:1].astype(jnp.float32)
        start = jnp.sum((key_ids < first_id).astype(jnp.float32)).astype(jnp.int32)
        starts.append(jnp.where(cycle_index >= distance, start, key_count))
    cols = pl.ds(0, rows)

    anything = functools.reduce(jnp.minimum, starts) < key_count

    @pl.when(jnp.logical_not(anything))
    def _():
        mixed_ref[...] = held_refs[0][...]
        large_ref[...] = held_refs[1][...]

    @pl.when(anything)
    def _():
        for i, chunk in enumerate(chunks):
            here = slice(i * key_count, (i + 1) * key_count)
            value_ref[:HEAD_DIM, here] = chunk[:key_count, HEAD_DIM:].T
        value_ref[HEAD_DIM:] = jnp.ones((TOTAL_ROWS, count * key_count), jnp.bfloat16)
        key_pos = lax.broadcasted_iota(jnp.int32, (key_count, 1), 0)
        biases = [jnp.where(key_pos >= start, 0.0, floor_score) for start in starts]
        column_valid = lax.broadcasted_iota(jnp.int32, (1, rows), 1) < run
        together = 2 if count == 1 else 1

        def one(step, carry):
            for u in range(together):
                h = step * together + u
                scores = [
                    jnp.dot(
                        chunk[:key_count, :HEAD_DIM],
                        turned_ref[h],
                        preferred_element_type=jnp.float32,
                    )
                    + bias
                    for chunk, bias in zip(chunks, biases)
                ]
                softmax_step(
                    scores, value_ref[...], held_refs, mixed_ref, large_ref, h, cols, column_valid
                )
            return carry

        lax.fori_loop(0, HEADS // together, one, 0)

    if final:
        part_ref = rest[2]
        stats = []
        for h in range(HEADS):
            total = mixed_ref[h, HEAD_DIM : HEAD_DIM + 1, :]
            part_ref[h * HEAD_DIM : (h + 1) * HEAD_DIM, :] = (
                mixed_ref[h, :HEAD_DIM, :] / total
            ).astype(jnp.bfloat16)
            left = large_ref[h] + jnp.log2(total)
            for _ in range(3):
                piece = left.astype(jnp.bfloat16)
                stats.append(piece.astype(jnp.float32))
                left = left - piece.astype(jnp.float32)
        stats.append(jnp.zeros((STAT_ROWS - 3 * HEADS, rows), jnp.float32))
        part_ref[HEADS * HEAD_DIM :, :] = jnp.concatenate(stats, axis=0).astype(jnp.bfloat16)


def merge_kernel(mixed_ref, large_ref, other_ref, out_ref):
    stats = other_ref[HEADS * HEAD_DIM :, :].astype(jnp.float32)
    for h in range(HEADS):
        total = mixed_ref[h, HEAD_DIM : HEAD_DIM + 1, :]
        large = large_ref[h] + jnp.log2(total)
        large_other = stats[3 * h : 3 * h + 1] + stats[3 * h + 1 : 3 * h + 2]
        large_other = large_other + stats[3 * h + 2 : 3 * h + 3]
        top = jnp.maximum(large, large_other)
        share = jnp.exp2(large - top)
        share_other = jnp.exp2(large_other - top)
        whole = share + share_other
        own = mixed_ref[h, :HEAD_DIM, :] * (share / (total * whole))
        other = other_ref[h * HEAD_DIM : (h + 1) * HEAD_DIM, :].astype(jnp.float32)
        joined = own + other * (share_other / whole)
        out_ref[:, h * HEAD_DIM : (h + 1) * HEAD_DIM] = joined.astype(jnp.bfloat16).T


def shards(query_rows, key_rows, value_rows, doc_ids):
    rows = query_rows.shape[0]
    key_count = key_rows.shape[0]
    devices = lax.axis_size("ctx")
    hop_count = min(11, devices // 4)
    ids = doc_ids.reshape(rows // 128, 128)
    value_rows_all = HEAD_DIM + TOTAL_ROWS

    packed = pl.pallas_call(
        pack_kernel,
        out_shape=jax.ShapeDtypeStruct((key_count + ID_ROWS, 2 * HEAD_DIM), jnp.bfloat16),
        in_specs=[VMEM] * 3,
        out_specs=VMEM,
        name="pack",
    )(key_rows, value_rows, ids)
    arrived = {
        d: lax.ppermute(packed, "ctx", [(i, (i + d) % devices) for i in range(devices)])
        for d in range(1, hop_count + 1)
    }
    mixed_shape = jax.ShapeDtypeStruct((HEADS, value_rows_all, rows), jnp.float32)
    large_shape = jax.ShapeDtypeStruct((HEADS, 1, rows), jnp.float32)
    turned, mixed, large = pl.pallas_call(
        own_kernel,
        out_shape=(
            jax.ShapeDtypeStruct((HEADS, HEAD_DIM, rows), jnp.bfloat16),
            mixed_shape,
            large_shape,
        ),
        in_specs=[VMEM] * 3,
        out_specs=(VMEM,) * 3,
        scratch_shapes=[
            pltpu.VMEM((value_rows_all, key_count), jnp.bfloat16),
            pltpu.VMEM((key_count, rows), jnp.float32),
        ],
        name="own",
    )(query_rows, packed, ids)
    near = list(range(1, hop_count))
    groups = [near[i : i + GROUP] for i in range(0, len(near), GROUP)] + [[hop_count]]
    for distances in groups:
        final = distances == groups[-1]
        outs = (mixed_shape, large_shape)
        if final:
            part_shape = (HEADS * HEAD_DIM + STAT_ROWS, rows)
            outs = outs + (jax.ShapeDtypeStruct(part_shape, jnp.bfloat16),)
        count = len(distances)
        mixed, large, *part = pl.pallas_call(
            functools.partial(behind_kernel, distances=tuple(distances), final=final),
            out_shape=outs,
            in_specs=[VMEM] * (4 + count),
            out_specs=(VMEM,) * len(outs),
            scratch_shapes=[pltpu.VMEM((value_rows_all, count * key_count), jnp.bfloat16)],
            input_output_aliases={2 + count: 0, 3 + count: 1},
            name=f"behind{distances[0]}",
        )(turned, ids, *[arrived[d] for d in distances], mixed, large)
    other = lax.ppermute(part[0], "kv", [(0, 1), (1, 0)])
    return pl.pallas_call(
        merge_kernel,
        out_shape=jax.ShapeDtypeStruct(query_rows.shape, jnp.bfloat16),
        in_specs=[VMEM] * 3,
        out_specs=VMEM,
        name="merge",
    )(mixed, large, other)


def solution(mesh):
    in_specs = (P("ctx", None), P(("ctx", "kv"), None), P(("ctx", "kv"), None), P("ctx"))
    out_specs = P("ctx", None)
    return jax.shard_map(shards, mesh=mesh, in_specs=in_specs, out_specs=out_specs, check_vma=False)
```

```python
import functools
import math

import jax
import jax.numpy as jnp
from jax import lax
from jax.experimental import pallas as pl
from jax.experimental.pallas import tpu as pltpu
from jax.sharding import PartitionSpec as P

HEADS = 8
HEAD_DIM = 128
ID_ROWS = 16
TOTAL_ROWS = 16
GROUP = 3
HALVES = 2
floor_score = -1e30
SCORE_SCALE = math.log2(math.e) / math.sqrt(HEAD_DIM)
HALF_HEADS = HEADS // HALVES
STAT_ROWS = 16


VMEM = pl.BlockSpec(memory_space=pltpu.VMEM)
ANY = pl.BlockSpec(memory_space=pl.ANY)
LIMITS = pltpu.CompilerParams(vmem_limit_bytes=24 << 20)


def near(value):
    return pltpu.with_memory_space_constraint(value, pltpu.VMEM)


def away(value):
    return pltpu.with_memory_space_constraint(value, pltpu.HBM)


def row_of(ids):
    return jnp.concatenate([ids[i : i + 1] for i in range(ids.shape[0])], axis=1)


def pack_kernel(key_in, value_in, ids_in, query_in, pack_ref, ids_ref, query_ref, sems):
    key_count = key_in.shape[0]
    copies = [
        pltpu.make_async_copy(ids_in, ids_ref, sems.at[0]),
        pltpu.make_async_copy(key_in, pack_ref.at[:key_count, :HEAD_DIM], sems.at[1]),
        pltpu.make_async_copy(value_in, pack_ref.at[:key_count, HEAD_DIM:], sems.at[2]),
        pltpu.make_async_copy(query_in, query_ref, sems.at[3]),
    ]
    for copy in copies:
        copy.start()
    copies[0].wait()
    lane_rows = key_count // 128
    ids = ids_ref[...]
    half = jnp.where(lax.axis_index("kv") == 0, ids[:lane_rows], ids[lane_rows : 2 * lane_rows])
    row = row_of(half).astype(jnp.float32).astype(jnp.bfloat16)
    pack_ref[key_count:, :] = jnp.broadcast_to(row, (ID_ROWS, key_count))
    for copy in copies[1:]:
        copy.wait()


def weights_of(scores, shift):
    blocks = [jnp.exp2(block * SCORE_SCALE - shift).astype(jnp.bfloat16) for block in scores]
    return jnp.concatenate(blocks, axis=0)


def largest_of(scores):
    tops = [jnp.max(block, axis=0, keepdims=True) for block in scores]
    return functools.reduce(jnp.maximum, tops) * SCORE_SCALE


def own_kernel(
    query_ref, pack_ref, ids_ref, again_ref, turned_ref, mixed_ref, large_ref, value_ref, bias_ref
):
    again_ref[...] = pack_ref[...]
    rows = query_ref.shape[0]
    key_count = pack_ref.shape[1]
    part_index = lax.axis_index("kv")
    for h in range(HEADS):
        turned_ref[h] = query_ref[:, h * HEAD_DIM : (h + 1) * HEAD_DIM].T
    value_ref[:HEAD_DIM] = pack_ref[:key_count, HEAD_DIM:].T
    value_ref[HEAD_DIM:] = jnp.ones((TOTAL_ROWS, key_count), jnp.bfloat16)
    token_ids = row_of(ids_ref[...].astype(jnp.float32))
    row = pack_ref[key_count:, :][:1].astype(jnp.float32)
    key_ids = jnp.broadcast_to(row, (128, key_count)).T[:, :1]
    token_pos = lax.broadcasted_iota(jnp.int32, (key_count, rows), 1)
    key_pos = lax.broadcasted_iota(jnp.int32, (key_count, rows), 0)
    key_pos = key_pos + part_index * key_count
    visible = (key_ids == token_ids) & (key_pos <= token_pos)
    bias_ref[...] = jnp.where(visible, 0.0, floor_score)

    def run(first, together):
        cols = slice(first, rows)

        def one(step, carry):
            for u in range(together):
                h = step * together + u
                scores = jnp.dot(
                    pack_ref[:key_count, :HEAD_DIM],
                    turned_ref[h, :, cols],
                    preferred_element_type=jnp.float32,
                )
                scores = [scores + bias_ref[:, cols]]
                largest = largest_of(scores)
                weights = weights_of(scores, largest)
                mixed_ref[h, :, cols] = jnp.dot(
                    value_ref[...], weights, preferred_element_type=jnp.float32
                )
                large_ref[h, :, cols] = largest
            return carry

        lax.fori_loop(0, HEADS // together, one, 0)

    @pl.when(part_index == 0)
    def _():
        run(0, 2)

    @pl.when(part_index > 0)
    def _():
        mixed_ref[:, :HEAD_DIM, :key_count] = jnp.zeros((HEADS, HEAD_DIM, key_count), jnp.float32)
        mixed_ref[:, HEAD_DIM:, :key_count] = jnp.ones((HEADS, TOTAL_ROWS, key_count), jnp.float32)
        large_ref[:, :, :key_count] = jnp.full((HEADS, 1, key_count), floor_score, jnp.float32)
        run(key_count, 4)


def behind_kernel(*refs, distances, first_head, lead, final):
    count = len(distances)
    turned_ref, ids_ref = refs[:2]
    chunks = refs[2 : 2 + count]
    rest = refs[2 + count :]
    if lead:
        held_mixed, held_large, mixed_ref, large_ref, value_ref = rest[:5]
        rest = rest[5:]
    else:
        value_ref, held_mixed, held_large, mixed_ref, large_ref = rest[:5]
        rest = rest[5:]
    rows = turned_ref.shape[2]
    key_count = chunks[0].shape[1]
    cycle_index = lax.axis_index("ctx")
    ids = ids_ref[...].astype(jnp.float32)
    first_id = jnp.min(ids)
    run = jnp.sum((ids == first_id).astype(jnp.float32)).astype(jnp.int32)
    starts = []
    for chunk, distance in zip(chunks, distances):
        key_ids = chunk[key_count:, :][:1].astype(jnp.float32)
        start = jnp.sum((key_ids < first_id).astype(jnp.float32)).astype(jnp.int32)
        starts.append(jnp.where(cycle_index >= distance, start, key_count))
    needed = jnp.int32(0)
    for i, start in enumerate(starts):
        needed = jnp.where(start < key_count, i + 1, needed)

    if lead:

        @pl.when(needed > 0)
        def _():
            for i, chunk in enumerate(chunks):
                here = slice(i * key_count, (i + 1) * key_count)
                value_ref[:HEAD_DIM, here] = chunk[:key_count, HEAD_DIM:].T
            value_ref[HEAD_DIM:] = jnp.ones((TOTAL_ROWS, count * key_count), jnp.bfloat16)

    key_pos = lax.broadcasted_iota(jnp.int32, (key_count, 1), 0)

    def attend(blocks, columns):
        column_valid = lax.broadcasted_iota(jnp.int32, (1, columns), 1) < run
        biases = [jnp.where(key_pos >= start, 0.0, floor_score) for start in starts[:blocks]]

        def one(step, carry):
            for u in range(2):
                h = first_head + step * 2 + u
                scores = [
                    jnp.dot(
                        chunk[:key_count, :HEAD_DIM],
                        turned_ref[h, :, :columns],
                        preferred_element_type=jnp.float32,
                    )
                    + bias
                    for chunk, bias in zip(chunks, biases)
                ]
                held = held_large[h, :, :columns]
                largest = jnp.where(column_valid, jnp.maximum(held, largest_of(scores)), held)
                weights = weights_of(scores, jnp.where(column_valid, largest, -floor_score))
                update = jnp.dot(
                    value_ref[:, : blocks * key_count], weights, preferred_element_type=jnp.float32
                )
                factor = jnp.exp2(held - largest)
                mixed_ref[h, :, :columns] = held_mixed[h, :, :columns] * factor + update
                large_ref[h, :, :columns] = largest
            return carry

        lax.fori_loop(0, HALF_HEADS // 2, one, 0)

    few = rows // 2
    sizes = sorted({min(2, count), max(count - 1, 1), count})
    for low, size in zip([0] + sizes, sizes):

        @pl.when((needed > low) & (needed <= size) & (run > few))
        def _(size=size):
            attend(size, rows)

    @pl.when((needed > 0) & (run <= few))
    def _():
        attend(count, few)

    if final:
        part_ref = rest[0]
        stats = []
        for u in range(HALF_HEADS):
            h = first_head + u
            total = mixed_ref[h, HEAD_DIM : HEAD_DIM + 1, :]
            part_ref[u * HEAD_DIM : (u + 1) * HEAD_DIM, :] = (
                mixed_ref[h, :HEAD_DIM, :] * (1.0 / total)
            ).astype(jnp.bfloat16)
            left = large_ref[h] + jnp.log2(total)
            for _ in range(3):
                piece = left.astype(jnp.bfloat16)
                stats.append(piece.astype(jnp.float32))
                left = left - piece.astype(jnp.float32)
        stats.append(jnp.zeros((STAT_ROWS - 3 * HALF_HEADS, rows), jnp.float32))
        part_ref[HALF_HEADS * HEAD_DIM :, :] = jnp.concatenate(stats, axis=0).astype(jnp.bfloat16)


def merge_kernel(*refs, first_head):
    mixed_ref, large_ref, other_ref = refs[:3]
    out_ref, out_vmem, sems = refs[-3:]
    copies = []
    stats = other_ref[HALF_HEADS * HEAD_DIM :, :].astype(jnp.float32)
    for u in range(HALF_HEADS):
        h = first_head + u
        total = mixed_ref[h, HEAD_DIM : HEAD_DIM + 1, :]
        large = large_ref[h] + jnp.log2(total)
        large_other = stats[3 * u : 3 * u + 1] + stats[3 * u + 1 : 3 * u + 2]
        large_other = large_other + stats[3 * u + 2 : 3 * u + 3]
        top = jnp.maximum(large, large_other)
        share = jnp.exp2(large - top)
        share_other = jnp.exp2(large_other - top)
        whole = share + share_other
        own = mixed_ref[h, :HEAD_DIM, :] * (share / (total * whole))
        other = other_ref[u * HEAD_DIM : (u + 1) * HEAD_DIM, :].astype(jnp.float32)
        joined = own + other * (share_other / whole)
        out_vmem[u] = joined.astype(jnp.bfloat16).T
        lanes = pl.ds(h * HEAD_DIM, HEAD_DIM)
        copies.append(pltpu.make_async_copy(out_vmem.at[u], out_ref.at[:, lanes], sems.at[u]))
        copies[-1].start()
    for copy in copies:
        copy.wait()


def shards(query_rows, key_rows, value_rows, doc_ids):
    rows = query_rows.shape[0]
    key_count = key_rows.shape[0]
    devices = lax.axis_size("ctx")
    hop_count = min(11, devices // 4)
    ids = doc_ids.reshape(rows // 128, 128)
    tall = HEAD_DIM + TOTAL_ROWS

    packed, ids, queries = pl.pallas_call(
        pack_kernel,
        out_shape=(
            pltpu.VMEM((key_count + ID_ROWS, 2 * HEAD_DIM), jnp.bfloat16),
            pltpu.VMEM(ids.shape, jnp.int32),
            pltpu.VMEM(query_rows.shape, jnp.bfloat16),
        ),
        in_specs=[ANY] * 4,
        out_specs=(VMEM,) * 3,
        scratch_shapes=[pltpu.SemaphoreType.DMA((4,))],
        compiler_params=LIMITS,
        name="pack",
    )(away(key_rows), away(value_rows), away(ids), away(query_rows))
    ids = near(ids)

    def from_behind(message, d):
        return near(lax.ppermute(message, "ctx", [(i, (i + d) % devices) for i in range(devices)]))

    arrived = {d: from_behind(packed, d) for d in range(hop_count - 1, 0, -1)}
    mixed_shape = pltpu.VMEM((HEADS, tall, rows), jnp.float32)
    large_shape = pltpu.VMEM((HEADS, 1, rows), jnp.float32)
    again, turned, mixed, large = pl.pallas_call(
        own_kernel,
        out_shape=(
            pltpu.VMEM(packed.shape, jnp.bfloat16),
            pltpu.VMEM((HEADS, HEAD_DIM, rows), jnp.bfloat16),
            mixed_shape,
            large_shape,
        ),
        in_specs=[VMEM] * 3,
        out_specs=(VMEM,) * 4,
        scratch_shapes=[
            pltpu.VMEM((tall, key_count), jnp.bfloat16),
            pltpu.VMEM((key_count, rows), jnp.float32),
        ],
        compiler_params=LIMITS,
        name="own",
    )(near(queries), near(packed), ids)
    turned = near(turned)
    arrived[hop_count] = from_behind(again, hop_count)
    closer = list(range(1, hop_count))
    groups = [closer[i : i + GROUP] for i in range(0, len(closer), GROUP)] + [[hop_count]]
    values = {}
    others = []
    part_shape = (HALF_HEADS * HEAD_DIM + STAT_ROWS, rows)
    for half in range(HALVES):
        for distances in groups:
            final = distances == groups[-1]
            lead = half == 0
            count = len(distances)
            chunks = [arrived[d] for d in distances]
            name = distances[0]
            outs = [mixed_shape, large_shape]
            extra = []
            if lead:
                outs.append(pltpu.VMEM((tall, count * key_count), jnp.bfloat16))
            else:
                extra = [near(values[name])]
            if final:
                outs.append(pltpu.VMEM(part_shape, jnp.bfloat16))
            place = 2 + count + len(extra)
            mixed, large, *more = pl.pallas_call(
                functools.partial(
                    behind_kernel,
                    distances=tuple(distances),
                    first_head=half * HALF_HEADS,
                    lead=lead,
                    final=final,
                ),
                out_shape=tuple(outs),
                in_specs=[VMEM] * (place + 2),
                out_specs=(VMEM,) * len(outs),
                input_output_aliases={place: 0, place + 1: 1},
                compiler_params=LIMITS,
                name=f"behind{name}_{half}",
            )(turned, ids, *chunks, *extra, near(mixed), near(large))
            if lead:
                values[name] = more[0]
        others.append(lax.ppermute(more[-1], "kv", [(0, 1), (1, 0)]))
    out = []
    for half in range(HALVES):
        out = [
            pl.pallas_call(
                functools.partial(merge_kernel, first_head=half * HALF_HEADS),
                out_shape=jax.ShapeDtypeStruct(query_rows.shape, jnp.bfloat16),
                in_specs=[VMEM] * 3 + [ANY] * len(out),
                out_specs=ANY,
                scratch_shapes=[
                    pltpu.VMEM((HALF_HEADS, rows, HEAD_DIM), jnp.bfloat16),
                    pltpu.SemaphoreType.DMA((HALF_HEADS,)),
                ],
                input_output_aliases={3: 0} if out else {},
                compiler_params=LIMITS,
                name=f"merge{half}",
            )(near(mixed), near(large), near(others[half]), *out)
        ]
    return out[0]


def solution(mesh):
    in_specs = (P("ctx", None), P(("ctx", "kv"), None), P(("ctx", "kv"), None), P("ctx"))
    out_specs = P("ctx", None)
    return jax.shard_map(shards, mesh=mesh, in_specs=in_specs, out_specs=out_specs, check_vma=False)
```

```python
import functools
import math

import jax
import jax.numpy as jnp
from jax import lax
from jax.experimental import pallas as pl
from jax.experimental.pallas import tpu as pltpu
from jax.sharding import PartitionSpec as P

HEADS = 8
HEAD_DIM = 128
ID_ROWS = 16
TOTAL_ROWS = 16
GROUP = 3
HALVES = 2
floor_score = -1e30
SCORE_SCALE = math.log2(math.e) / math.sqrt(HEAD_DIM)
HALF_HEADS = HEADS // HALVES
STAT_ROWS = 16


VMEM = pl.BlockSpec(memory_space=pltpu.VMEM)
ANY = pl.BlockSpec(memory_space=pl.ANY)
LIMITS = pltpu.CompilerParams(vmem_limit_bytes=24 << 20)


def near(value):
    return pltpu.with_memory_space_constraint(value, pltpu.VMEM)


def away(value):
    return pltpu.with_memory_space_constraint(value, pltpu.HBM)


def row_of(ids):
    return jnp.concatenate([ids[i : i + 1] for i in range(ids.shape[0])], axis=1)


def pack_kernel(key_in, value_in, ids_in, query_in, pack_ref, ids_ref, query_ref, sems):
    key_count = key_in.shape[0]
    copies = [
        pltpu.make_async_copy(ids_in, ids_ref, sems.at[0]),
        pltpu.make_async_copy(key_in, pack_ref.at[:key_count, :HEAD_DIM], sems.at[1]),
        pltpu.make_async_copy(value_in, pack_ref.at[:key_count, HEAD_DIM:], sems.at[2]),
        pltpu.make_async_copy(query_in, query_ref, sems.at[3]),
    ]
    for copy in copies:
        copy.start()
    copies[0].wait()
    lane_rows = key_count // 128
    ids = ids_ref[...]
    half = jnp.where(lax.axis_index("kv") == 0, ids[:lane_rows], ids[lane_rows : 2 * lane_rows])
    row = row_of(half).astype(jnp.float32).astype(jnp.bfloat16)
    pack_ref[key_count:, :] = jnp.broadcast_to(row, (ID_ROWS, key_count))
    for copy in copies[1:]:
        copy.wait()


def again_kernel(pack_ref, large_ref, again_ref):
    again_ref[...] = pack_ref[...]


def weights_of(scores, shift):
    blocks = [jnp.exp2(block * SCORE_SCALE - shift).astype(jnp.bfloat16) for block in scores]
    return jnp.concatenate(blocks, axis=0)


def largest_of(scores):
    tops = [jnp.max(block, axis=0, keepdims=True) for block in scores]
    return functools.reduce(jnp.maximum, tops) * SCORE_SCALE


def in_turn(heads, score, weigh, mix):
    current = score(heads[0])
    pending = None
    for u, h in enumerate(heads):
        following = score(heads[u + 1]) if u + 1 < len(heads) else None
        if pending is not None:
            mix(*pending)
        pending = (h, *weigh(h, *current))
        current = following
    mix(*pending)


def own_kernel(
    query_ref, pack_ref, ids_ref, turned_ref, mixed_ref, large_ref, value_ref, bias_ref
):
    rows = query_ref.shape[0]
    key_count = pack_ref.shape[1]
    part_index = lax.axis_index("kv")
    for h in range(HEADS):
        turned_ref[h] = query_ref[:, h * HEAD_DIM : (h + 1) * HEAD_DIM].T
    value_ref[:HEAD_DIM] = pack_ref[:key_count, HEAD_DIM:].T
    value_ref[HEAD_DIM:] = jnp.ones((TOTAL_ROWS, key_count), jnp.bfloat16)
    token_ids = row_of(ids_ref[...].astype(jnp.float32))
    row = pack_ref[key_count:, :][:1].astype(jnp.float32)
    key_ids = jnp.broadcast_to(row, (128, key_count)).T[:, :1]
    token_pos = lax.broadcasted_iota(jnp.int32, (key_count, rows), 1)
    key_pos = lax.broadcasted_iota(jnp.int32, (key_count, rows), 0)
    key_pos = key_pos + part_index * key_count
    visible = (key_ids == token_ids) & (key_pos <= token_pos)
    bias_ref[...] = jnp.where(visible, 0.0, floor_score)

    def run(first):
        cols = slice(first, rows)

        def score(h):
            scores = jnp.dot(
                pack_ref[:key_count, :HEAD_DIM],
                turned_ref[h, :, cols],
                preferred_element_type=jnp.float32,
            )
            scores = [scores + bias_ref[:, cols]]
            return scores, largest_of(scores)

        def weigh(h, scores, largest):
            large_ref[h, :, cols] = largest
            return (weights_of(scores, largest),)

        def mix(h, weights):
            mixed_ref[h, :, cols] = jnp.dot(
                value_ref[...], weights, preferred_element_type=jnp.float32
            )

        in_turn(range(HEADS), score, weigh, mix)

    @pl.when(part_index == 0)
    def _():
        run(0)

    @pl.when(part_index > 0)
    def _():
        mixed_ref[:, :HEAD_DIM, :key_count] = jnp.zeros((HEADS, HEAD_DIM, key_count), jnp.float32)
        mixed_ref[:, HEAD_DIM:, :key_count] = jnp.ones((HEADS, TOTAL_ROWS, key_count), jnp.float32)
        large_ref[:, :, :key_count] = jnp.full((HEADS, 1, key_count), floor_score, jnp.float32)
        run(key_count)


def behind_kernel(*refs, distances, heads, keep, kept, final):
    count = len(distances)
    turned_ref, ids_ref = refs[:2]
    chunks = refs[2 : 2 + count]
    rest = list(refs[2 + count :])
    if kept:
        value_ref = rest.pop(0)
    held_mixed, held_large, mixed_ref, large_ref = rest[:4]
    rest = rest[4:]
    if not kept:
        value_ref = rest.pop(0) if keep else rest.pop()
    rows = turned_ref.shape[2]
    key_count = chunks[0].shape[1]
    cycle_index = lax.axis_index("ctx")
    ids = ids_ref[...].astype(jnp.float32)
    first_id = jnp.min(ids)
    run = jnp.sum((ids == first_id).astype(jnp.float32)).astype(jnp.int32)
    starts = []
    for chunk, distance in zip(chunks, distances):
        key_ids = chunk[key_count:, :][:1].astype(jnp.float32)
        start = jnp.sum((key_ids < first_id).astype(jnp.float32)).astype(jnp.int32)
        starts.append(jnp.where(cycle_index >= distance, start, key_count))
    needed = jnp.int32(0)
    for i, start in enumerate(starts):
        needed = jnp.where(start < key_count, i + 1, needed)

    if not kept:

        @pl.when(needed > 0)
        def _():
            for i, chunk in enumerate(chunks):
                here = slice(i * key_count, (i + 1) * key_count)
                value_ref[:HEAD_DIM, here] = chunk[:key_count, HEAD_DIM:].T
            value_ref[HEAD_DIM:] = jnp.ones((TOTAL_ROWS, count * key_count), jnp.bfloat16)

    key_pos = lax.broadcasted_iota(jnp.int32, (key_count, 1), 0)

    def attend(blocks, columns):
        column_valid = lax.broadcasted_iota(jnp.int32, (1, columns), 1) < run
        biases = [jnp.where(key_pos >= start, 0.0, floor_score) for start in starts[:blocks]]

        def score(h):
            scores = [
                jnp.dot(
                    chunk[:key_count, :HEAD_DIM],
                    turned_ref[h, :, :columns],
                    preferred_element_type=jnp.float32,
                )
                + bias
                for chunk, bias in zip(chunks, biases)
            ]
            return scores, largest_of(scores)

        def weigh(h, scores, largest):
            held = held_large[h, :, :columns]
            largest = jnp.where(column_valid, jnp.maximum(held, largest), held)
            large_ref[h, :, :columns] = largest
            weights = weights_of(scores, jnp.where(column_valid, largest, -floor_score))
            return weights, jnp.exp2(held - largest)

        def mix(h, weights, factor):
            update = jnp.dot(
                value_ref[:, : blocks * key_count], weights, preferred_element_type=jnp.float32
            )
            mixed_ref[h, :, :columns] = held_mixed[h, :, :columns] * factor + update

        in_turn(heads, score, weigh, mix)

    few = rows // 2
    sizes = sorted({max(count - 1, 1), count})
    for low, size in zip([0] + sizes, sizes):

        @pl.when((needed > low) & (needed <= size) & (run > few))
        def _(size=size):
            attend(size, rows)

    @pl.when((needed > 0) & (run <= few))
    def _():
        attend(count, few)

    if final:
        part_ref = rest[0]
        stats = []
        for u, h in enumerate(heads):
            total = mixed_ref[h, HEAD_DIM : HEAD_DIM + 1, :]
            part_ref[u * HEAD_DIM : (u + 1) * HEAD_DIM, :] = (
                mixed_ref[h, :HEAD_DIM, :] * (1.0 / total)
            ).astype(jnp.bfloat16)
            left = large_ref[h] + jnp.log2(total)
            for _ in range(3):
                piece = left.astype(jnp.bfloat16)
                stats.append(piece.astype(jnp.float32))
                left = left - piece.astype(jnp.float32)
        stats.append(jnp.zeros((STAT_ROWS - 3 * HALF_HEADS, rows), jnp.float32))
        part_ref[HALF_HEADS * HEAD_DIM :, :] = jnp.concatenate(stats, axis=0).astype(jnp.bfloat16)


def merge_kernel(*refs, first_head):
    mixed_ref, large_ref, other_ref = refs[:3]
    out_ref, out_vmem, sems = refs[-3:]
    copies = []
    stats = other_ref[HALF_HEADS * HEAD_DIM :, :].astype(jnp.float32)
    for u in range(HALF_HEADS):
        h = first_head + u
        total = mixed_ref[h, HEAD_DIM : HEAD_DIM + 1, :]
        large = large_ref[h] + jnp.log2(total)
        large_other = stats[3 * u : 3 * u + 1] + stats[3 * u + 1 : 3 * u + 2]
        large_other = large_other + stats[3 * u + 2 : 3 * u + 3]
        top = jnp.maximum(large, large_other)
        share = jnp.exp2(large - top)
        share_other = jnp.exp2(large_other - top)
        whole = share + share_other
        own = mixed_ref[h, :HEAD_DIM, :] * (share / (total * whole))
        other = other_ref[u * HEAD_DIM : (u + 1) * HEAD_DIM, :].astype(jnp.float32)
        joined = own + other * (share_other / whole)
        out_vmem[u] = joined.astype(jnp.bfloat16).T
        lanes = pl.ds(h * HEAD_DIM, HEAD_DIM)
        copies.append(pltpu.make_async_copy(out_vmem.at[u], out_ref.at[:, lanes], sems.at[u]))
        copies[-1].start()
    for copy in copies:
        copy.wait()


def shards(query_rows, key_rows, value_rows, doc_ids):
    rows = query_rows.shape[0]
    key_count = key_rows.shape[0]
    devices = lax.axis_size("ctx")
    hop_count = min(11, devices // 4)
    ids = doc_ids.reshape(rows // 128, 128)
    tall = HEAD_DIM + TOTAL_ROWS

    packed, ids, queries = pl.pallas_call(
        pack_kernel,
        out_shape=(
            pltpu.VMEM((key_count + ID_ROWS, 2 * HEAD_DIM), jnp.bfloat16),
            pltpu.VMEM(ids.shape, jnp.int32),
            pltpu.VMEM(query_rows.shape, jnp.bfloat16),
        ),
        in_specs=[ANY] * 4,
        out_specs=(VMEM,) * 3,
        scratch_shapes=[pltpu.SemaphoreType.DMA((4,))],
        compiler_params=LIMITS,
        name="pack",
    )(away(key_rows), away(value_rows), away(ids), away(query_rows))
    ids = near(ids)

    def from_behind(message, d):
        return near(lax.ppermute(message, "ctx", [(i, (i + d) % devices) for i in range(devices)]))

    arrived = {d: from_behind(packed, d) for d in range(hop_count - 1, 0, -1)}
    mixed_shape = pltpu.VMEM((HEADS, tall, rows), jnp.float32)
    large_shape = pltpu.VMEM((HEADS, 1, rows), jnp.float32)
    turned, mixed, large = pl.pallas_call(
        own_kernel,
        out_shape=(
            pltpu.VMEM((HEADS, HEAD_DIM, rows), jnp.bfloat16),
            mixed_shape,
            large_shape,
        ),
        in_specs=[VMEM] * 3,
        out_specs=(VMEM,) * 3,
        scratch_shapes=[
            pltpu.VMEM((tall, key_count), jnp.bfloat16),
            pltpu.VMEM((key_count, rows), jnp.float32),
        ],
        compiler_params=LIMITS,
        name="own",
    )(near(queries), near(packed), ids)
    turned = near(turned)
    again = pl.pallas_call(
        again_kernel,
        out_shape=pltpu.VMEM(packed.shape, jnp.bfloat16),
        in_specs=[VMEM] * 2,
        out_specs=VMEM,
        compiler_params=LIMITS,
        name="again",
    )(near(packed), near(large))
    arrived[hop_count] = from_behind(again, hop_count)
    part_shape = (HALF_HEADS * HEAD_DIM + STAT_ROWS, rows)
    state = (mixed, large)

    def behind(state, distances, heads, final=False, keep=False, kept=None):
        count = len(distances)
        value_shape = pltpu.VMEM((tall, count * key_count), jnp.bfloat16)
        extra = [] if kept is None else [near(kept)]
        outs = [mixed_shape, large_shape]
        scratch = []
        if keep:
            outs.append(value_shape)
        elif kept is None:
            scratch.append(value_shape)
        if final:
            outs.append(pltpu.VMEM(part_shape, jnp.bfloat16))
        place = 2 + count + len(extra)
        mixed, large, *more = pl.pallas_call(
            functools.partial(
                behind_kernel,
                distances=distances,
                heads=heads,
                keep=keep,
                kept=kept is not None,
                final=final,
            ),
            out_shape=tuple(outs),
            in_specs=[VMEM] * (place + 2),
            out_specs=(VMEM,) * len(outs),
            scratch_shapes=scratch,
            input_output_aliases={place: 0, place + 1: 1},
            compiler_params=LIMITS,
            name=f"behind{distances[0]}_{heads.start}",
        )(turned, ids, *[arrived[d] for d in distances], *extra, near(state[0]), near(state[1]))
        return (mixed, large), more

    middle = list(range(2, hop_count))
    for i in range(0, len(middle), GROUP):
        state, _ = behind(state, tuple(middle[i : i + GROUP]), range(HEADS))
    values = {}
    others = []
    for half in range(HALVES):
        heads = range(half * HALF_HEADS, (half + 1) * HALF_HEADS)
        for d in (1, hop_count):
            first = half == 0
            state, more = behind(
                state,
                (d,),
                heads,
                final=d == hop_count,
                keep=first,
                kept=None if first else values[d],
            )
            if first:
                values[d] = more.pop(0)
        others.append(lax.ppermute(more[0], "kv", [(0, 1), (1, 0)]))
    mixed, large = state
    out = []
    for half in range(HALVES):
        out = [
            pl.pallas_call(
                functools.partial(merge_kernel, first_head=half * HALF_HEADS),
                out_shape=jax.ShapeDtypeStruct(query_rows.shape, jnp.bfloat16),
                in_specs=[VMEM] * 3 + [ANY] * len(out),
                out_specs=ANY,
                scratch_shapes=[
                    pltpu.VMEM((HALF_HEADS, rows, HEAD_DIM), jnp.bfloat16),
                    pltpu.SemaphoreType.DMA((HALF_HEADS,)),
                ],
                input_output_aliases={3: 0} if out else {},
                compiler_params=LIMITS,
                name=f"merge{half}",
            )(near(mixed), near(large), near(others[half]), *out)
        ]
    return out[0]


def solution(mesh):
    in_specs = (P("ctx", None), P(("ctx", "kv"), None), P(("ctx", "kv"), None), P("ctx"))
    out_specs = P("ctx", None)
    return jax.shard_map(shards, mesh=mesh, in_specs=in_specs, out_specs=out_specs, check_vma=False)
```

```python
import functools
import math

import jax
import jax.numpy as jnp
from jax import lax
from jax.experimental import pallas as pl
from jax.experimental.pallas import tpu as pltpu
from jax.sharding import PartitionSpec as P

HEADS = 8
HEAD_DIM = 128
ID_ROWS = 8
TOTAL_ROWS = 16
GROUP = 3
SPLIT = (5, 3)
floor_score = -1e30
SCORE_SCALE = math.log2(math.e) / math.sqrt(HEAD_DIM)
STAT_ROWS = 16


VMEM = pl.BlockSpec(memory_space=pltpu.VMEM)
ANY = pl.BlockSpec(memory_space=pl.ANY)
LIMITS = pltpu.CompilerParams(vmem_limit_bytes=24 << 20)


def near(value):
    return pltpu.with_memory_space_constraint(value, pltpu.VMEM)


def away(value):
    return pltpu.with_memory_space_constraint(value, pltpu.HBM)


def row_of(ids):
    return jnp.concatenate([ids[i : i + 1] for i in range(ids.shape[0])], axis=1)


def pack_kernel(key_in, value_in, ids_in, pack_ref, ids_ref, sems):
    key_count = key_in.shape[0]
    copies = [
        pltpu.make_async_copy(ids_in, ids_ref, sems.at[0]),
        pltpu.make_async_copy(key_in, pack_ref.at[:key_count, :HEAD_DIM], sems.at[1]),
        pltpu.make_async_copy(value_in, pack_ref.at[:key_count, HEAD_DIM:], sems.at[2]),
    ]
    for copy in copies:
        copy.start()
    copies[0].wait()
    lane_rows = key_count // 128
    ids = ids_ref[...]
    half = jnp.where(lax.axis_index("kv") == 0, ids[:lane_rows], ids[lane_rows : 2 * lane_rows])
    row = row_of(half).astype(jnp.float32).astype(jnp.bfloat16)
    pack_ref[key_count:, :] = jnp.broadcast_to(row, (ID_ROWS, key_count))
    for copy in copies[1:]:
        copy.wait()


def relay_kernel(pack_ref, arrived_ref, large_ref, relay_ref, *, block):
    lowest = lax.axis_index("ctx") % block < block // 2

    @pl.when(lowest)
    def _():
        relay_ref[...] = pack_ref[...]

    @pl.when(jnp.logical_not(lowest))
    def _():
        relay_ref[...] = arrived_ref[...]


def weights_of(scores, shift):
    blocks = [jnp.exp2(block * SCORE_SCALE - shift).astype(jnp.bfloat16) for block in scores]
    return jnp.concatenate(blocks, axis=0)


def largest_of(scores):
    tops = [jnp.max(block, axis=0, keepdims=True) for block in scores]
    return functools.reduce(jnp.maximum, tops) * SCORE_SCALE


def in_turn(heads, score, weigh, mix):
    current = score(heads[0])
    pending = None
    for u, h in enumerate(heads):
        following = score(heads[u + 1]) if u + 1 < len(heads) else None
        if pending is not None:
            mix(*pending)
        pending = (h, *weigh(h, *current))
        current = following
    mix(*pending)


def own_kernel(
    query_in,
    pack_ref,
    ids_ref,
    turned_ref,
    mixed_ref,
    large_ref,
    value_ref,
    bias_ref,
    query_ref,
    sems,
):
    rows = query_in.shape[0]
    copies = []
    for h in range(HEADS):
        lanes = slice(h * HEAD_DIM, (h + 1) * HEAD_DIM)
        copies.append(
            pltpu.make_async_copy(query_in.at[:, lanes], query_ref.at[:, lanes], sems.at[h])
        )
        copies[-1].start()
    key_count = pack_ref.shape[1]
    part_index = lax.axis_index("kv")
    value_ref[:HEAD_DIM] = pack_ref[:key_count, HEAD_DIM:].T
    value_ref[HEAD_DIM:] = jnp.ones((TOTAL_ROWS, key_count), jnp.bfloat16)
    token_ids = row_of(ids_ref[...].astype(jnp.float32))
    row = pack_ref[key_count:, :][:1].astype(jnp.float32)
    key_ids = jnp.broadcast_to(row, (128, key_count)).T[:, :1]
    token_pos = lax.broadcasted_iota(jnp.int32, (key_count, rows), 1)
    key_pos = lax.broadcasted_iota(jnp.int32, (key_count, rows), 0)
    key_pos = key_pos + part_index * key_count
    visible = (key_ids == token_ids) & (key_pos <= token_pos)
    bias_ref[...] = jnp.where(visible, 0.0, floor_score)
    for h in range(HEADS):
        copies[h].wait()
        turned_ref[h] = query_ref[:, h * HEAD_DIM : (h + 1) * HEAD_DIM].T

    def run(first):
        cols = slice(first, rows)

        def score(h):
            scores = jnp.dot(
                pack_ref[:key_count, :HEAD_DIM],
                turned_ref[h, :, cols],
                preferred_element_type=jnp.float32,
            )
            scores = [scores + bias_ref[:, cols]]
            return scores, largest_of(scores)

        def weigh(h, scores, largest):
            large_ref[h, :, cols] = largest
            return (weights_of(scores, largest),)

        def mix(h, weights):
            mixed_ref[h, :, cols] = jnp.dot(
                value_ref[...], weights, preferred_element_type=jnp.float32
            )

        in_turn(range(HEADS), score, weigh, mix)

    @pl.when(part_index == 0)
    def _():
        run(0)

    @pl.when(part_index > 0)
    def _():
        mixed_ref[:, :HEAD_DIM, :key_count] = jnp.zeros((HEADS, HEAD_DIM, key_count), jnp.float32)
        mixed_ref[:, HEAD_DIM:, :key_count] = jnp.ones((HEADS, TOTAL_ROWS, key_count), jnp.float32)
        large_ref[:, :, :key_count] = jnp.full((HEADS, 1, key_count), floor_score, jnp.float32)
        run(key_count)


def behind_kernel(*refs, distances, heads, keep, kept, final):
    count = len(distances)
    turned_ref, ids_ref = refs[:2]
    chunks = refs[2 : 2 + count]
    rest = list(refs[2 + count :])
    if kept:
        value_ref = rest.pop(0)
    held_mixed, held_large, mixed_ref, large_ref = rest[:4]
    rest = rest[4:]
    if not kept:
        value_ref = rest.pop(0) if keep else rest.pop()
    rows = turned_ref.shape[2]
    key_count = chunks[0].shape[1]
    cycle_index = lax.axis_index("ctx")
    ids = ids_ref[...].astype(jnp.float32)
    first_id = jnp.min(ids)
    run = jnp.sum((ids == first_id).astype(jnp.float32)).astype(jnp.int32)
    starts = []
    for chunk, distance in zip(chunks, distances):
        key_ids = chunk[key_count:, :][:1].astype(jnp.float32)
        start = jnp.sum((key_ids < first_id).astype(jnp.float32)).astype(jnp.int32)
        starts.append(jnp.where(cycle_index >= distance, start, key_count))
    needed = jnp.int32(0)
    for i, start in enumerate(starts):
        needed = jnp.where(start < key_count, i + 1, needed)

    if not kept:

        @pl.when(needed > 0)
        def _():
            for i, chunk in enumerate(chunks):
                here = slice(i * key_count, (i + 1) * key_count)
                value_ref[:HEAD_DIM, here] = chunk[:key_count, HEAD_DIM:].T
            value_ref[HEAD_DIM:] = jnp.ones((TOTAL_ROWS, count * key_count), jnp.bfloat16)

    key_pos = lax.broadcasted_iota(jnp.int32, (key_count, 1), 0)

    def attend(blocks, columns):
        column_valid = lax.broadcasted_iota(jnp.int32, (1, columns), 1) < run
        biases = [jnp.where(key_pos >= start, 0.0, floor_score) for start in starts[:blocks]]

        def score(h):
            scores = [
                jnp.dot(
                    chunk[:key_count, :HEAD_DIM],
                    turned_ref[h, :, :columns],
                    preferred_element_type=jnp.float32,
                )
                + bias
                for chunk, bias in zip(chunks, biases)
            ]
            return scores, largest_of(scores)

        def weigh(h, scores, largest):
            held = held_large[h, :, :columns]
            largest = jnp.where(column_valid, jnp.maximum(held, largest), held)
            large_ref[h, :, :columns] = largest
            weights = weights_of(scores, jnp.where(column_valid, largest, -floor_score))
            return weights, jnp.exp2(held - largest)

        def mix(h, weights, factor):
            update = jnp.dot(
                value_ref[:, : blocks * key_count], weights, preferred_element_type=jnp.float32
            )
            mixed_ref[h, :, :columns] = held_mixed[h, :, :columns] * factor + update

        in_turn(heads, score, weigh, mix)

    few = rows // 2
    sizes = sorted({max(count - 1, 1), count})
    for low, size in zip([0] + sizes, sizes):

        @pl.when((needed > low) & (needed <= size) & (run > few))
        def _(size=size):
            attend(size, rows)

    @pl.when((needed > 0) & (run <= few))
    def _():
        attend(count, few)

    if final:
        part_ref = rest[0]
        stats = []
        for u, h in enumerate(heads):
            total = mixed_ref[h, HEAD_DIM : HEAD_DIM + 1, :]
            part_ref[u * HEAD_DIM : (u + 1) * HEAD_DIM, :] = (
                mixed_ref[h, :HEAD_DIM, :] * (1.0 / total)
            ).astype(jnp.bfloat16)
            left = large_ref[h] + jnp.log2(total)
            for _ in range(3):
                piece = left.astype(jnp.bfloat16)
                stats.append(piece.astype(jnp.float32))
                left = left - piece.astype(jnp.float32)
        stats.append(jnp.zeros((STAT_ROWS - 3 * len(heads), rows), jnp.float32))
        part_ref[len(heads) * HEAD_DIM :, :] = jnp.concatenate(stats, axis=0).astype(jnp.bfloat16)


def merge_kernel(*refs, heads):
    mixed_ref, large_ref, other_ref = refs[:3]
    out_ref, out_vmem, sems = refs[-3:]
    copies = []
    stats = other_ref[len(heads) * HEAD_DIM :, :].astype(jnp.float32)
    for u, h in enumerate(heads):
        total = mixed_ref[h, HEAD_DIM : HEAD_DIM + 1, :]
        large = large_ref[h] + jnp.log2(total)
        large_other = stats[3 * u : 3 * u + 1] + stats[3 * u + 1 : 3 * u + 2]
        large_other = large_other + stats[3 * u + 2 : 3 * u + 3]
        top = jnp.maximum(large, large_other)
        share = jnp.exp2(large - top)
        share_other = jnp.exp2(large_other - top)
        whole = share + share_other
        own = mixed_ref[h, :HEAD_DIM, :] * (share / (total * whole))
        other = other_ref[u * HEAD_DIM : (u + 1) * HEAD_DIM, :].astype(jnp.float32)
        joined = own + other * (share_other / whole)
        out_vmem[u] = joined.astype(jnp.bfloat16).T
        lanes = pl.ds(h * HEAD_DIM, HEAD_DIM)
        copies.append(pltpu.make_async_copy(out_vmem.at[u], out_ref.at[:, lanes], sems.at[u]))
        copies[-1].start()
    for copy in copies:
        copy.wait()


def shards(query_rows, key_rows, value_rows, doc_ids):
    rows = query_rows.shape[0]
    key_count = key_rows.shape[0]
    devices = lax.axis_size("ctx")
    hop_count = min(11, devices // 4)
    ids = doc_ids.reshape(rows // 128, 128)
    tall = HEAD_DIM + TOTAL_ROWS

    packed, ids = pl.pallas_call(
        pack_kernel,
        out_shape=(
            pltpu.VMEM((key_count + ID_ROWS, 2 * HEAD_DIM), jnp.bfloat16),
            pltpu.VMEM(ids.shape, jnp.int32),
        ),
        in_specs=[ANY] * 3,
        out_specs=(VMEM,) * 2,
        scratch_shapes=[pltpu.SemaphoreType.DMA((3,))],
        compiler_params=LIMITS,
        name="pack",
    )(away(key_rows), away(value_rows), away(ids))
    ids = near(ids)

    block = 1 << (hop_count.bit_length() - 1)

    def sent(message, route):
        return near(lax.ppermute(message, "ctx", route))

    def behind_by(d):
        return [(i, (i + d) % devices) for i in range(devices)]

    arrived = {block: sent(packed, behind_by(block))}
    for d in range(1, hop_count + 1):
        if d not in (block // 2, block):
            arrived[d] = sent(packed, behind_by(d))
    mixed_shape = pltpu.VMEM((HEADS, tall, rows), jnp.float32)
    large_shape = pltpu.VMEM((HEADS, 1, rows), jnp.float32)
    turned, mixed, large = pl.pallas_call(
        own_kernel,
        out_shape=(
            pltpu.VMEM((HEADS, HEAD_DIM, rows), jnp.bfloat16),
            mixed_shape,
            large_shape,
        ),
        in_specs=[ANY, VMEM, VMEM],
        out_specs=(VMEM,) * 3,
        scratch_shapes=[
            pltpu.VMEM((tall, key_count), jnp.bfloat16),
            pltpu.VMEM((key_count, rows), jnp.float32),
            pltpu.VMEM(query_rows.shape, jnp.bfloat16),
            pltpu.SemaphoreType.DMA((HEADS,)),
        ],
        compiler_params=LIMITS,
        name="own",
    )(away(query_rows), near(packed), ids)
    turned = near(turned)
    relayed = pl.pallas_call(
        functools.partial(relay_kernel, block=block),
        out_shape=pltpu.VMEM(packed.shape, jnp.bfloat16),
        in_specs=[VMEM] * 3,
        out_specs=VMEM,
        compiler_params=LIMITS,
        name="relay",
    )(near(packed), arrived[block], near(large))
    across = [(i, i ^ (block // 2)) for i in range(devices)]
    arrived[block // 2] = sent(relayed, across)
    state = (mixed, large)

    def behind(state, distances, heads, final=False, keep=False, kept=None):
        count = len(distances)
        value_shape = pltpu.VMEM((tall, count * key_count), jnp.bfloat16)
        extra = [] if kept is None else [near(kept)]
        outs = [mixed_shape, large_shape]
        scratch = []
        if keep:
            outs.append(value_shape)
        elif kept is None:
            scratch.append(value_shape)
        if final:
            part_shape = (len(heads) * HEAD_DIM + STAT_ROWS, rows)
            outs.append(pltpu.VMEM(part_shape, jnp.bfloat16))
        place = 2 + count + len(extra)
        mixed, large, *more = pl.pallas_call(
            functools.partial(
                behind_kernel,
                distances=distances,
                heads=heads,
                keep=keep,
                kept=kept is not None,
                final=final,
            ),
            out_shape=tuple(outs),
            in_specs=[VMEM] * (place + 2),
            out_specs=(VMEM,) * len(outs),
            scratch_shapes=scratch,
            input_output_aliases={place: 0, place + 1: 1},
            compiler_params=LIMITS,
            name=f"behind{distances[0]}_{heads.start}",
        )(turned, ids, *[arrived[d] for d in distances], *extra, near(state[0]), near(state[1]))
        return (mixed, large), more

    others = [d for d in range(2, hop_count + 1) if d not in (block // 2, block)]
    late = tuple(sorted((block // 2, others.pop(0))))
    early = [(1, block)] + [tuple(others[i : i + GROUP]) for i in range(0, len(others), GROUP)]
    for distances in early:
        state, _ = behind(state, distances, range(HEADS))
    values = None
    others = []
    shares = [range(sum(SPLIT[:i]), sum(SPLIT[: i + 1])) for i in range(len(SPLIT))]
    for heads in shares:
        state, more = behind(
            state, late, heads, final=True, keep=values is None, kept=values
        )
        if values is None:
            values = more.pop(0)
        others.append(lax.ppermute(more[0], "kv", [(0, 1), (1, 0)]))
    mixed, large = state
    out = []
    for heads, other in zip(shares, others):
        out = [
            pl.pallas_call(
                functools.partial(merge_kernel, heads=heads),
                out_shape=jax.ShapeDtypeStruct(query_rows.shape, jnp.bfloat16),
                in_specs=[VMEM] * 3 + [ANY] * len(out),
                out_specs=ANY,
                scratch_shapes=[
                    pltpu.VMEM((len(heads), rows, HEAD_DIM), jnp.bfloat16),
                    pltpu.SemaphoreType.DMA((len(heads),)),
                ],
                input_output_aliases={3: 0} if out else {},
                compiler_params=LIMITS,
                name=f"merge{heads.start}",
            )(near(mixed), near(large), near(other), *out)
        ]
    return out[0]


def solution(mesh):
    in_specs = (P("ctx", None), P(("ctx", "kv"), None), P(("ctx", "kv"), None), P("ctx"))
    out_specs = P("ctx", None)
    return jax.shard_map(shards, mesh=mesh, in_specs=in_specs, out_specs=out_specs, check_vma=False)
```

```python
import functools
import math

import jax
import jax.numpy as jnp
from jax import lax
from jax.experimental import pallas as pl
from jax.experimental.pallas import tpu as pltpu
from jax.sharding import PartitionSpec as P

HEADS = 8
HEAD_DIM = 128
ID_ROWS = 8
TOTAL_ROWS = 16
GROUP = 3
SPLIT = (5, 3)
floor_score = -1e30
SCORE_SCALE = math.log2(math.e) / math.sqrt(HEAD_DIM)
STAT_ROWS = 16


VMEM = pl.BlockSpec(memory_space=pltpu.VMEM)
ANY = pl.BlockSpec(memory_space=pl.ANY)
LIMITS = pltpu.CompilerParams(vmem_limit_bytes=24 << 20)


def near(value):
    return pltpu.with_memory_space_constraint(value, pltpu.VMEM)


def away(value):
    return pltpu.with_memory_space_constraint(value, pltpu.HBM)


def row_of(ids):
    return jnp.concatenate([ids[i : i + 1] for i in range(ids.shape[0])], axis=1)


def pack_kernel(key_in, value_in, ids_in, pack_ref, ids_ref, sems):
    key_count = key_in.shape[0]
    copies = [
        pltpu.make_async_copy(ids_in, ids_ref, sems.at[0]),
        pltpu.make_async_copy(key_in, pack_ref.at[:key_count, :HEAD_DIM], sems.at[1]),
        pltpu.make_async_copy(value_in, pack_ref.at[:key_count, HEAD_DIM:], sems.at[2]),
    ]
    for copy in copies:
        copy.start()
    copies[0].wait()
    lane_rows = key_count // 128
    ids = ids_ref[...]
    half = jnp.where(lax.axis_index("kv") == 0, ids[:lane_rows], ids[lane_rows : 2 * lane_rows])
    row = row_of(half).astype(jnp.float32).astype(jnp.bfloat16)
    pack_ref[key_count:, :] = jnp.broadcast_to(row, (ID_ROWS, key_count))
    for copy in copies[1:]:
        copy.wait()


def relay_kernel(pack_ref, arrived_ref, large_ref, relay_ref, *, block):
    lowest = lax.axis_index("ctx") % block < block // 2

    @pl.when(lowest)
    def _():
        relay_ref[...] = pack_ref[...]

    @pl.when(jnp.logical_not(lowest))
    def _():
        relay_ref[...] = arrived_ref[...]


def weights_of(scores, shift):
    blocks = [jnp.exp2(block * SCORE_SCALE - shift).astype(jnp.bfloat16) for block in scores]
    return jnp.concatenate(blocks, axis=0)


def largest_of(scores):
    tops = [jnp.max(block, axis=0, keepdims=True) for block in scores]
    return functools.reduce(jnp.maximum, tops) * SCORE_SCALE


def in_turn(heads, score, weigh, mix):
    current = score(heads[0])
    pending = None
    for u, h in enumerate(heads):
        following = score(heads[u + 1]) if u + 1 < len(heads) else None
        if pending is not None:
            mix(*pending)
        pending = (h, *weigh(h, *current))
        current = following
    mix(*pending)


def own_kernel(
    query_in,
    pack_ref,
    ids_ref,
    turned_ref,
    mixed_ref,
    large_ref,
    value_ref,
    bias_ref,
    query_ref,
    sem,
):
    rows = query_in.shape[0]
    copy = pltpu.make_async_copy(query_in, query_ref, sem)
    copy.start()
    key_count = pack_ref.shape[1]
    part_index = lax.axis_index("kv")
    value_ref[:HEAD_DIM] = pack_ref[:key_count, HEAD_DIM:].T
    value_ref[HEAD_DIM:] = jnp.ones((TOTAL_ROWS, key_count), jnp.bfloat16)
    token_ids = row_of(ids_ref[...].astype(jnp.float32))
    row = pack_ref[key_count:, :][:1].astype(jnp.float32)
    key_ids = jnp.broadcast_to(row, (128, key_count)).T[:, :1]
    token_pos = lax.broadcasted_iota(jnp.int32, (key_count, rows), 1)
    key_pos = lax.broadcasted_iota(jnp.int32, (key_count, rows), 0)
    key_pos = key_pos + part_index * key_count
    visible = (key_ids == token_ids) & (key_pos <= token_pos)
    bias_ref[...] = jnp.where(visible, 0.0, floor_score)
    copy.wait()
    for h in range(HEADS):
        turned_ref[h] = query_ref[:, h * HEAD_DIM : (h + 1) * HEAD_DIM].T

    def run(first):
        cols = slice(first, rows)

        def score(h):
            scores = jnp.dot(
                pack_ref[:key_count, :HEAD_DIM],
                turned_ref[h, :, cols],
                preferred_element_type=jnp.float32,
            )
            scores = [scores + bias_ref[:, cols]]
            return scores, largest_of(scores)

        def weigh(h, scores, largest):
            large_ref[h, :, cols] = largest
            return (weights_of(scores, largest),)

        def mix(h, weights):
            mixed_ref[h, :, cols] = jnp.dot(
                value_ref[...], weights, preferred_element_type=jnp.float32
            )

        in_turn(range(HEADS), score, weigh, mix)

    @pl.when(part_index == 0)
    def _():
        run(0)

    @pl.when(part_index > 0)
    def _():
        mixed_ref[:, :HEAD_DIM, :key_count] = jnp.zeros((HEADS, HEAD_DIM, key_count), jnp.float32)
        mixed_ref[:, HEAD_DIM:, :key_count] = jnp.ones((HEADS, TOTAL_ROWS, key_count), jnp.float32)
        large_ref[:, :, :key_count] = jnp.full((HEADS, 1, key_count), floor_score, jnp.float32)
        run(key_count)


def behind_kernel(*refs, distances, heads, keep, kept, final):
    count = len(distances)
    turned_ref, ids_ref = refs[:2]
    chunks = refs[2 : 2 + count]
    rest = list(refs[2 + count :])
    if kept:
        value_ref = rest.pop(0)
    held_mixed, held_large, mixed_ref, large_ref = rest[:4]
    rest = rest[4:]
    if not kept:
        value_ref = rest.pop(0) if keep else rest.pop()
    rows = turned_ref.shape[2]
    key_count = chunks[0].shape[1]
    cycle_index = lax.axis_index("ctx")
    ids = ids_ref[...].astype(jnp.float32)
    first_id = ids[:1, :1]
    run = jnp.sum((ids == first_id).astype(jnp.float32)).astype(jnp.int32)
    starts = []
    for chunk, distance in zip(chunks, distances):
        key_ids = chunk[key_count:, :][:1].astype(jnp.float32)
        start = jnp.sum((key_ids < first_id).astype(jnp.float32)).astype(jnp.int32)
        starts.append(jnp.where(cycle_index >= distance, start, key_count))
    needed = jnp.int32(0)
    for i, start in enumerate(starts):
        needed = jnp.where(start < key_count, i + 1, needed)

    if not kept:

        @pl.when(needed > 0)
        def _():
            for i, chunk in enumerate(chunks):
                here = slice(i * key_count, (i + 1) * key_count)
                value_ref[:HEAD_DIM, here] = chunk[:key_count, HEAD_DIM:].T
            value_ref[HEAD_DIM:] = jnp.ones((TOTAL_ROWS, count * key_count), jnp.bfloat16)

    key_pos = lax.broadcasted_iota(jnp.int32, (key_count, 1), 0)

    def attend(blocks, columns):
        column_valid = lax.broadcasted_iota(jnp.int32, (1, columns), 1) < run
        biases = [jnp.where(key_pos >= start, 0.0, floor_score) for start in starts[:blocks]]

        def score(h):
            scores = [
                jnp.dot(
                    chunk[:key_count, :HEAD_DIM],
                    turned_ref[h, :, :columns],
                    preferred_element_type=jnp.float32,
                )
                + bias
                for chunk, bias in zip(chunks, biases)
            ]
            return scores, largest_of(scores)

        def weigh(h, scores, largest):
            held = held_large[h, :, :columns]
            largest = jnp.where(column_valid, jnp.maximum(held, largest), held)
            large_ref[h, :, :columns] = largest
            weights = weights_of(scores, jnp.where(column_valid, largest, -floor_score))
            return weights, jnp.exp2(held - largest)

        def mix(h, weights, factor):
            update = jnp.dot(
                value_ref[:, : blocks * key_count], weights, preferred_element_type=jnp.float32
            )
            mixed_ref[h, :, :columns] = held_mixed[h, :, :columns] * factor + update

        in_turn(heads, score, weigh, mix)

    few = rows // 2
    sizes = sorted({max(count - 1, 1), count})
    for low, size in zip([0] + sizes, sizes):

        @pl.when((needed > low) & (needed <= size) & (run > few))
        def _(size=size):
            attend(size, rows)

    @pl.when((needed > 0) & (run <= few))
    def _():
        attend(count, few)

    if final:
        part_ref = rest[0]
        stats = []
        for u, h in enumerate(heads):
            total = mixed_ref[h, HEAD_DIM : HEAD_DIM + 1, :]
            part_ref[u * HEAD_DIM : (u + 1) * HEAD_DIM, :] = (
                mixed_ref[h, :HEAD_DIM, :] * (1.0 / total)
            ).astype(jnp.bfloat16)
            left = large_ref[h] + jnp.log2(total)
            for _ in range(3):
                piece = left.astype(jnp.bfloat16)
                stats.append(piece.astype(jnp.float32))
                left = left - piece.astype(jnp.float32)
        stats.append(jnp.zeros((STAT_ROWS - 3 * len(heads), rows), jnp.float32))
        part_ref[len(heads) * HEAD_DIM :, :] = jnp.concatenate(stats, axis=0).astype(jnp.bfloat16)


def merge_kernel(*refs, heads):
    mixed_ref, large_ref, other_ref = refs[:3]
    out_ref, out_vmem, sems = refs[-3:]
    copies = []
    stats = other_ref[len(heads) * HEAD_DIM :, :].astype(jnp.float32)
    for u, h in enumerate(heads):
        total = mixed_ref[h, HEAD_DIM : HEAD_DIM + 1, :]
        large = large_ref[h] + jnp.log2(total)
        large_other = stats[3 * u : 3 * u + 1] + stats[3 * u + 1 : 3 * u + 2]
        large_other = large_other + stats[3 * u + 2 : 3 * u + 3]
        top = jnp.maximum(large, large_other)
        share = jnp.exp2(large - top)
        share_other = jnp.exp2(large_other - top)
        whole = share + share_other
        own = mixed_ref[h, :HEAD_DIM, :] * (share / (total * whole))
        other = other_ref[u * HEAD_DIM : (u + 1) * HEAD_DIM, :].astype(jnp.float32)
        joined = own + other * (share_other / whole)
        out_vmem[u] = joined.astype(jnp.bfloat16).T
        lanes = pl.ds(h * HEAD_DIM, HEAD_DIM)
        copies.append(pltpu.make_async_copy(out_vmem.at[u], out_ref.at[:, lanes], sems.at[u]))
        copies[-1].start()
    for copy in copies:
        copy.wait()


def shards(query_rows, key_rows, value_rows, doc_ids):
    rows = query_rows.shape[0]
    key_count = key_rows.shape[0]
    devices = lax.axis_size("ctx")
    hop_count = min(11, devices // 4)
    ids = doc_ids.reshape(rows // 128, 128)
    tall = HEAD_DIM + TOTAL_ROWS

    packed, ids = pl.pallas_call(
        pack_kernel,
        out_shape=(
            pltpu.VMEM((key_count + ID_ROWS, 2 * HEAD_DIM), jnp.bfloat16),
            pltpu.VMEM(ids.shape, jnp.int32),
        ),
        in_specs=[ANY] * 3,
        out_specs=(VMEM,) * 2,
        scratch_shapes=[pltpu.SemaphoreType.DMA((3,))],
        compiler_params=LIMITS,
        name="pack",
    )(away(key_rows), away(value_rows), away(ids))
    ids = near(ids)

    block = 1 << (hop_count.bit_length() - 1)

    def sent(message, route):
        return near(lax.ppermute(message, "ctx", route))

    def behind_by(d):
        return [(i, (i + d) % devices) for i in range(devices)]

    arrived = {block: sent(packed, behind_by(block))}
    for d in range(1, hop_count + 1):
        if d not in (block // 2, block):
            arrived[d] = sent(packed, behind_by(d))
    mixed_shape = pltpu.VMEM((HEADS, tall, rows), jnp.float32)
    large_shape = pltpu.VMEM((HEADS, 1, rows), jnp.float32)
    turned, mixed, large = pl.pallas_call(
        own_kernel,
        out_shape=(
            pltpu.VMEM((HEADS, HEAD_DIM, rows), jnp.bfloat16),
            mixed_shape,
            large_shape,
        ),
        in_specs=[ANY, VMEM, VMEM],
        out_specs=(VMEM,) * 3,
        scratch_shapes=[
            pltpu.VMEM((tall, key_count), jnp.bfloat16),
            pltpu.VMEM((key_count, rows), jnp.float32),
            pltpu.VMEM(query_rows.shape, jnp.bfloat16),
            pltpu.SemaphoreType.DMA,
        ],
        compiler_params=LIMITS,
        name="own",
    )(away(query_rows), near(packed), ids)
    turned = near(turned)
    relayed = pl.pallas_call(
        functools.partial(relay_kernel, block=block),
        out_shape=pltpu.VMEM(packed.shape, jnp.bfloat16),
        in_specs=[VMEM] * 3,
        out_specs=VMEM,
        compiler_params=LIMITS,
        name="relay",
    )(near(packed), arrived[block], near(large))
    across = [(i, i ^ (block // 2)) for i in range(devices)]
    arrived[block // 2] = sent(relayed, across)
    state = (mixed, large)

    def behind(state, distances, heads, final=False, keep=False, kept=None):
        count = len(distances)
        value_shape = pltpu.VMEM((tall, count * key_count), jnp.bfloat16)
        extra = [] if kept is None else [near(kept)]
        outs = [mixed_shape, large_shape]
        scratch = []
        if keep:
            outs.append(value_shape)
        elif kept is None:
            scratch.append(value_shape)
        if final:
            part_shape = (len(heads) * HEAD_DIM + STAT_ROWS, rows)
            outs.append(pltpu.VMEM(part_shape, jnp.bfloat16))
        place = 2 + count + len(extra)
        mixed, large, *more = pl.pallas_call(
            functools.partial(
                behind_kernel,
                distances=distances,
                heads=heads,
                keep=keep,
                kept=kept is not None,
                final=final,
            ),
            out_shape=tuple(outs),
            in_specs=[VMEM] * (place + 2),
            out_specs=(VMEM,) * len(outs),
            scratch_shapes=scratch,
            input_output_aliases={place: 0, place + 1: 1},
            compiler_params=LIMITS,
            name=f"behind{distances[0]}_{heads.start}",
        )(turned, ids, *[arrived[d] for d in distances], *extra, near(state[0]), near(state[1]))
        return (mixed, large), more

    others = [d for d in range(2, hop_count + 1) if d not in (block // 2, block)]
    late = tuple(sorted((block // 2, others.pop(0))))
    early = [(1, block)] + [tuple(others[i : i + GROUP]) for i in range(0, len(others), GROUP)]
    for distances in early:
        state, _ = behind(state, distances, range(HEADS))
    values = None
    others = []
    shares = [range(sum(SPLIT[:i]), sum(SPLIT[: i + 1])) for i in range(len(SPLIT))]
    for heads in shares:
        state, more = behind(
            state, late, heads, final=True, keep=values is None, kept=values
        )
        if values is None:
            values = more.pop(0)
        others.append(lax.ppermute(more[0], "kv", [(0, 1), (1, 0)]))
    mixed, large = state
    out = []
    for heads, other in zip(shares, others):
        out = [
            pl.pallas_call(
                functools.partial(merge_kernel, heads=heads),
                out_shape=jax.ShapeDtypeStruct(query_rows.shape, jnp.bfloat16),
                in_specs=[VMEM] * 3 + [ANY] * len(out),
                out_specs=ANY,
                scratch_shapes=[
                    pltpu.VMEM((len(heads), rows, HEAD_DIM), jnp.bfloat16),
                    pltpu.SemaphoreType.DMA((len(heads),)),
                ],
                input_output_aliases={3: 0} if out else {},
                compiler_params=LIMITS,
                name=f"merge{heads.start}",
            )(near(mixed), near(large), near(other), *out)
        ]
    return out[0]


def solution(mesh):
    in_specs = (P("ctx", None), P(("ctx", "kv"), None), P(("ctx", "kv"), None), P("ctx"))
    out_specs = P("ctx", None)
    return jax.shard_map(shards, mesh=mesh, in_specs=in_specs, out_specs=out_specs, check_vma=False)
```

```python
import functools
import math

import jax
import jax.numpy as jnp
from jax import lax
from jax.experimental import pallas as pl
from jax.experimental.pallas import tpu as pltpu
from jax.sharding import PartitionSpec as P

HEADS = 8
HEAD_DIM = 128
ID_ROWS = 8
TOTAL_ROWS = 16
GROUP = 3
SPLIT = (5, 3)
floor_score = -1e30
SCORE_SCALE = math.log2(math.e) / math.sqrt(HEAD_DIM)
STAT_ROWS = 16


VMEM = pl.BlockSpec(memory_space=pltpu.VMEM)
ANY = pl.BlockSpec(memory_space=pl.ANY)
LIMITS = pltpu.CompilerParams(vmem_limit_bytes=24 << 20)


def near(value):
    return pltpu.with_memory_space_constraint(value, pltpu.VMEM)


def away(value):
    return pltpu.with_memory_space_constraint(value, pltpu.HBM)


def row_of(ids):
    return jnp.concatenate([ids[i : i + 1] for i in range(ids.shape[0])], axis=1)


def pack_kernel(key_in, value_in, ids_in, pack_ref, ids_ref, sems):
    key_count = key_in.shape[0]
    copies = [
        pltpu.make_async_copy(ids_in, ids_ref, sems.at[0]),
        pltpu.make_async_copy(key_in, pack_ref.at[:key_count, :HEAD_DIM], sems.at[1]),
        pltpu.make_async_copy(value_in, pack_ref.at[:key_count, HEAD_DIM:], sems.at[2]),
    ]
    for copy in copies:
        copy.start()
    copies[0].wait()
    lane_rows = key_count // 128
    ids = ids_ref[...]
    half = jnp.where(lax.axis_index("kv") == 0, ids[:lane_rows], ids[lane_rows : 2 * lane_rows])
    row = row_of(half).astype(jnp.float32).astype(jnp.bfloat16)
    pack_ref[key_count:, :] = jnp.broadcast_to(row, (ID_ROWS, key_count))
    for copy in copies[1:]:
        copy.wait()


def relay_kernel(pack_ref, arrived_ref, large_ref, relay_ref, *, block):
    lowest = lax.axis_index("ctx") % block < block // 2

    @pl.when(lowest)
    def _():
        relay_ref[...] = pack_ref[...]

    @pl.when(jnp.logical_not(lowest))
    def _():
        relay_ref[...] = arrived_ref[...]


def weights_of(scores, shift):
    blocks = [jnp.exp2(block * SCORE_SCALE - shift).astype(jnp.bfloat16) for block in scores]
    return jnp.concatenate(blocks, axis=0)


def largest_of(scores):
    tops = [jnp.max(block, axis=0, keepdims=True) for block in scores]
    return functools.reduce(jnp.maximum, tops) * SCORE_SCALE


def in_turn(heads, score, weigh, mix):
    current = score(heads[0])
    pending = None
    for u, h in enumerate(heads):
        following = score(heads[u + 1]) if u + 1 < len(heads) else None
        if pending is not None:
            mix(*pending)
        pending = (h, *weigh(h, *current))
        current = following
    mix(*pending)


def own_kernel(
    query_in,
    pack_ref,
    ids_ref,
    turned_ref,
    mixed_ref,
    large_ref,
    value_ref,
    bias_ref,
    query_ref,
    sem,
):
    rows = query_in.shape[0]
    copy = pltpu.make_async_copy(query_in, query_ref, sem)
    copy.start()
    key_count = pack_ref.shape[1]
    part_index = lax.axis_index("kv")
    value_ref[:HEAD_DIM] = pack_ref[:key_count, HEAD_DIM:].T
    value_ref[HEAD_DIM:] = jnp.ones((TOTAL_ROWS, key_count), jnp.bfloat16)
    token_ids = row_of(ids_ref[...].astype(jnp.float32))
    row = pack_ref[key_count:, :][:1].astype(jnp.float32)
    key_ids = jnp.broadcast_to(row, (128, key_count)).T[:, :1]
    token_pos = lax.broadcasted_iota(jnp.int32, (key_count, rows), 1)
    key_pos = lax.broadcasted_iota(jnp.int32, (key_count, rows), 0)
    key_pos = key_pos + part_index * key_count
    visible = (key_ids == token_ids) & (key_pos <= token_pos)
    bias_ref[...] = jnp.where(visible, 0.0, floor_score)
    copy.wait()
    for h in range(HEADS):
        turned_ref[h] = query_ref[:, h * HEAD_DIM : (h + 1) * HEAD_DIM].T

    def run(first):
        cols = slice(first, rows)

        def score(h):
            scores = jnp.dot(
                pack_ref[:key_count, :HEAD_DIM],
                turned_ref[h, :, cols],
                preferred_element_type=jnp.float32,
            )
            scores = [scores + bias_ref[:, cols]]
            return scores, largest_of(scores)

        def weigh(h, scores, largest):
            large_ref[h, :, cols] = largest
            return (weights_of(scores, largest),)

        def mix(h, weights):
            mixed_ref[h, :, cols] = jnp.dot(
                value_ref[...], weights, preferred_element_type=jnp.float32
            )

        in_turn(range(HEADS), score, weigh, mix)

    @pl.when(part_index == 0)
    def _():
        run(0)

    @pl.when(part_index > 0)
    def _():
        mixed_ref[:, :HEAD_DIM, :key_count] = jnp.zeros((HEADS, HEAD_DIM, key_count), jnp.float32)
        mixed_ref[:, HEAD_DIM:, :key_count] = jnp.ones((HEADS, TOTAL_ROWS, key_count), jnp.float32)
        large_ref[:, :, :key_count] = jnp.full((HEADS, 1, key_count), floor_score, jnp.float32)
        run(key_count)


def behind_kernel(*refs, distances, heads, keep, kept, final):
    count = len(distances)
    turned_ref, ids_ref = refs[:2]
    chunks = refs[2 : 2 + count]
    rest = list(refs[2 + count :])
    if kept:
        value_ref = rest.pop(0)
    held_mixed, held_large, mixed_ref, large_ref = rest[:4]
    rest = rest[4:]
    if not kept:
        value_ref = rest.pop(0) if keep else rest.pop()
    rows = turned_ref.shape[2]
    key_count = chunks[0].shape[1]
    cycle_index = lax.axis_index("ctx")
    ids = ids_ref[...].astype(jnp.float32)
    first_id = ids[:1, :1]
    run = jnp.sum((ids == first_id).astype(jnp.float32)).astype(jnp.int32)
    starts = []
    for chunk, distance in zip(chunks, distances):
        key_ids = chunk[key_count:, :][:1].astype(jnp.float32)
        start = jnp.sum((key_ids < first_id).astype(jnp.float32)).astype(jnp.int32)
        starts.append(jnp.where(cycle_index >= distance, start, key_count))
    needed = jnp.int32(0)
    for i, start in enumerate(starts):
        needed = jnp.where(start < key_count, i + 1, needed)

    if not kept:

        @pl.when(needed > 0)
        def _():
            for i, chunk in enumerate(chunks):
                here = slice(i * key_count, (i + 1) * key_count)

                @pl.when(needed > i)
                def _(chunk=chunk, here=here):
                    value_ref[:HEAD_DIM, here] = chunk[:key_count, HEAD_DIM:].T

                @pl.when(needed <= i)
                def _(here=here):
                    value_ref[:HEAD_DIM, here] = jnp.zeros((HEAD_DIM, key_count), jnp.bfloat16)

            value_ref[HEAD_DIM:] = jnp.ones((TOTAL_ROWS, count * key_count), jnp.bfloat16)

    key_pos = lax.broadcasted_iota(jnp.int32, (key_count, 1), 0)

    def attend(blocks, columns):
        column_valid = lax.broadcasted_iota(jnp.int32, (1, columns), 1) < run
        biases = [jnp.where(key_pos >= start, 0.0, floor_score) for start in starts[:blocks]]

        def score(h):
            scores = [
                jnp.dot(
                    chunk[:key_count, :HEAD_DIM],
                    turned_ref[h, :, :columns],
                    preferred_element_type=jnp.float32,
                )
                + bias
                for chunk, bias in zip(chunks, biases)
            ]
            return scores, largest_of(scores)

        def weigh(h, scores, largest):
            held = held_large[h, :, :columns]
            largest = jnp.where(column_valid, jnp.maximum(held, largest), held)
            large_ref[h, :, :columns] = largest
            weights = weights_of(scores, jnp.where(column_valid, largest, -floor_score))
            return weights, jnp.exp2(held - largest)

        def mix(h, weights, factor):
            update = jnp.dot(
                value_ref[:, : blocks * key_count], weights, preferred_element_type=jnp.float32
            )
            mixed_ref[h, :, :columns] = held_mixed[h, :, :columns] * factor + update

        in_turn(heads, score, weigh, mix)

    few = rows // 2
    sizes = sorted({max(count - 1, 1), count})
    for low, size in zip([0] + sizes, sizes):

        @pl.when((needed > low) & (needed <= size) & (run > few))
        def _(size=size):
            attend(size, rows)

    @pl.when((needed > 0) & (run <= few))
    def _():
        attend(count, few)

    if final:
        part_ref = rest[0]
        stats = []
        for u, h in enumerate(heads):
            total = mixed_ref[h, HEAD_DIM : HEAD_DIM + 1, :]
            part_ref[u * HEAD_DIM : (u + 1) * HEAD_DIM, :] = (
                mixed_ref[h, :HEAD_DIM, :] * (1.0 / total)
            ).astype(jnp.bfloat16)
            left = large_ref[h] + jnp.log2(total)
            for _ in range(3):
                piece = left.astype(jnp.bfloat16)
                stats.append(piece.astype(jnp.float32))
                left = left - piece.astype(jnp.float32)
        stats.append(jnp.zeros((STAT_ROWS - 3 * len(heads), rows), jnp.float32))
        part_ref[len(heads) * HEAD_DIM :, :] = jnp.concatenate(stats, axis=0).astype(jnp.bfloat16)


def merge_kernel(*refs, heads):
    mixed_ref, large_ref, other_ref = refs[:3]
    out_ref, out_vmem, sems = refs[-3:]
    copies = []
    stats = other_ref[len(heads) * HEAD_DIM :, :].astype(jnp.float32)
    for u, h in enumerate(heads):
        total = mixed_ref[h, HEAD_DIM : HEAD_DIM + 1, :]
        large = large_ref[h] + jnp.log2(total)
        large_other = stats[3 * u : 3 * u + 1] + stats[3 * u + 1 : 3 * u + 2]
        large_other = large_other + stats[3 * u + 2 : 3 * u + 3]
        top = jnp.maximum(large, large_other)
        share = jnp.exp2(large - top)
        share_other = jnp.exp2(large_other - top)
        whole = share + share_other
        own = mixed_ref[h, :HEAD_DIM, :] * (share / (total * whole))
        other = other_ref[u * HEAD_DIM : (u + 1) * HEAD_DIM, :].astype(jnp.float32)
        joined = own + other * (share_other / whole)
        out_vmem[u] = joined.astype(jnp.bfloat16).T
        lanes = pl.ds(h * HEAD_DIM, HEAD_DIM)
        copies.append(pltpu.make_async_copy(out_vmem.at[u], out_ref.at[:, lanes], sems.at[u]))
        copies[-1].start()
    for copy in copies:
        copy.wait()


def shards(query_rows, key_rows, value_rows, doc_ids):
    rows = query_rows.shape[0]
    key_count = key_rows.shape[0]
    devices = lax.axis_size("ctx")
    hop_count = min(11, devices // 4)
    ids = doc_ids.reshape(rows // 128, 128)
    tall = HEAD_DIM + TOTAL_ROWS

    packed, ids = pl.pallas_call(
        pack_kernel,
        out_shape=(
            pltpu.VMEM((key_count + ID_ROWS, 2 * HEAD_DIM), jnp.bfloat16),
            pltpu.VMEM(ids.shape, jnp.int32),
        ),
        in_specs=[ANY] * 3,
        out_specs=(VMEM,) * 2,
        scratch_shapes=[pltpu.SemaphoreType.DMA((3,))],
        compiler_params=LIMITS,
        name="pack",
    )(away(key_rows), away(value_rows), away(ids))
    ids = near(ids)

    block = 1 << (hop_count.bit_length() - 1)

    def sent(message, route):
        return near(lax.ppermute(message, "ctx", route))

    def behind_by(d):
        return [(i, (i + d) % devices) for i in range(devices)]

    arrived = {block: sent(packed, behind_by(block))}
    for d in range(1, hop_count + 1):
        if d not in (block // 2, block):
            arrived[d] = sent(packed, behind_by(d))
    mixed_shape = pltpu.VMEM((HEADS, tall, rows), jnp.float32)
    large_shape = pltpu.VMEM((HEADS, 1, rows), jnp.float32)
    turned, mixed, large = pl.pallas_call(
        own_kernel,
        out_shape=(
            pltpu.VMEM((HEADS, HEAD_DIM, rows), jnp.bfloat16),
            mixed_shape,
            large_shape,
        ),
        in_specs=[ANY, VMEM, VMEM],
        out_specs=(VMEM,) * 3,
        scratch_shapes=[
            pltpu.VMEM((tall, key_count), jnp.bfloat16),
            pltpu.VMEM((key_count, rows), jnp.float32),
            pltpu.VMEM(query_rows.shape, jnp.bfloat16),
            pltpu.SemaphoreType.DMA,
        ],
        compiler_params=LIMITS,
        name="own",
    )(away(query_rows), near(packed), ids)
    turned = near(turned)
    relayed = pl.pallas_call(
        functools.partial(relay_kernel, block=block),
        out_shape=pltpu.VMEM(packed.shape, jnp.bfloat16),
        in_specs=[VMEM] * 3,
        out_specs=VMEM,
        compiler_params=LIMITS,
        name="relay",
    )(near(packed), arrived[block], near(large))
    across = [(i, i ^ (block // 2)) for i in range(devices)]
    arrived[block // 2] = sent(relayed, across)
    state = (mixed, large)

    def behind(state, distances, heads, final=False, keep=False, kept=None):
        count = len(distances)
        value_shape = pltpu.VMEM((tall, count * key_count), jnp.bfloat16)
        extra = [] if kept is None else [near(kept)]
        outs = [mixed_shape, large_shape]
        scratch = []
        if keep:
            outs.append(value_shape)
        elif kept is None:
            scratch.append(value_shape)
        if final:
            part_shape = (len(heads) * HEAD_DIM + STAT_ROWS, rows)
            outs.append(pltpu.VMEM(part_shape, jnp.bfloat16))
        place = 2 + count + len(extra)
        mixed, large, *more = pl.pallas_call(
            functools.partial(
                behind_kernel,
                distances=distances,
                heads=heads,
                keep=keep,
                kept=kept is not None,
                final=final,
            ),
            out_shape=tuple(outs),
            in_specs=[VMEM] * (place + 2),
            out_specs=(VMEM,) * len(outs),
            scratch_shapes=scratch,
            input_output_aliases={place: 0, place + 1: 1},
            compiler_params=LIMITS,
            name=f"behind{distances[0]}_{heads.start}",
        )(turned, ids, *[arrived[d] for d in distances], *extra, near(state[0]), near(state[1]))
        return (mixed, large), more

    others = [d for d in range(2, hop_count + 1) if d not in (block // 2, block)]
    late = tuple(sorted((block // 2, others.pop(0))))
    early = [(1, block)] + [tuple(others[i : i + GROUP]) for i in range(0, len(others), GROUP)]
    for distances in early:
        state, _ = behind(state, distances, range(HEADS))
    values = None
    others = []
    shares = [range(sum(SPLIT[:i]), sum(SPLIT[: i + 1])) for i in range(len(SPLIT))]
    for heads in shares:
        state, more = behind(
            state, late, heads, final=True, keep=values is None, kept=values
        )
        if values is None:
            values = more.pop(0)
        others.append(lax.ppermute(more[0], "kv", [(0, 1), (1, 0)]))
    mixed, large = state
    out = []
    for heads, other in zip(shares, others):
        out = [
            pl.pallas_call(
                functools.partial(merge_kernel, heads=heads),
                out_shape=jax.ShapeDtypeStruct(query_rows.shape, jnp.bfloat16),
                in_specs=[VMEM] * 3 + [ANY] * len(out),
                out_specs=ANY,
                scratch_shapes=[
                    pltpu.VMEM((len(heads), rows, HEAD_DIM), jnp.bfloat16),
                    pltpu.SemaphoreType.DMA((len(heads),)),
                ],
                input_output_aliases={3: 0} if out else {},
                compiler_params=LIMITS,
                name=f"merge{heads.start}",
            )(near(mixed), near(large), near(other), *out)
        ]
    return out[0]


def solution(mesh):
    in_specs = (P("ctx", None), P(("ctx", "kv"), None), P(("ctx", "kv"), None), P("ctx"))
    out_specs = P("ctx", None)
    return jax.shard_map(shards, mesh=mesh, in_specs=in_specs, out_specs=out_specs, check_vma=False)
```
